32 devices in a mesh: mem: 2 (over x), lat: 4 (over z), lon: 4 (over y, core).
Axes of the slice: x: 2, y: 2, z: 4, core: 2. Of those that a mesh axis runs over, the one named last changes fastest.
Arguments:
- control: bfloat16 [8, 256, 128, 128], P('mem', 'lat', 'lon'), may hold values from -21 to 21
- ensemble: bfloat16 [8, 256, 128, 128], P('mem', 'lat', 'lon'), may hold values from -3 to 3
- precision: float32 [256, 128, 128], P('lat', 'lon'), may hold values from 0.5 to 8
- lat_taps: float32 [9], replicated, may hold values from 0.05 to 0.3
- lon_taps: float32 [9], replicated, may hold values from 0.05 to 0.3
- vertical: bfloat16 [128, 128], replicated, may hold values from -0.5 to 0.5
Outputs:
- hessian: float32 [8, 256, 128, 128], P('mem', 'lat', 'lon')
- curvature: float32 [], replicated
The draws below stay inside these ranges and needn't reach their ends.
All inputs are finite; a program needn't handle non-finite values.
Results may differ from the reference program's by a relative error of at most 0.0038.
Values may be sent and summed in bfloat16 or wider, within the bound.
A program may use at most 64 MiB of HBM per device.

```python
import math
import jax
import jax.numpy as jnp
from jax import lax

LV = 128
TAPS = 9
MEMBERS = 8
NLAT = 256
NLON = 128


def draw_control(key, part):
    first_key = jax.random.fold_in(jax.random.fold_in(key, 11), 0)
    shape = (MEMBERS, NLAT, NLON, LV)
    member_pos = jnp.arange(MEMBERS, dtype=jnp.float32) / max(MEMBERS - 1, 1)
    lat_pos = jnp.arange(NLAT, dtype=jnp.float32) / max(NLAT - 1, 1)
    lon_pos = jnp.arange(NLON, dtype=jnp.float32) / max(NLON - 1, 1)
    exponent = member_pos[:, None, None, None] + lat_pos[None, :, None, None] + lon_pos[None, None, :, None]
    scaling = jnp.exp(0.5 * jnp.log(3.0) * exponent)
    base = jax.random.normal(first_key, shape, jnp.float32)
    base = jnp.clip(base, -4.0, 4.0)
    return (base * scaling).astype(jnp.bfloat16)


def block_scale(stream_key, dims, cuts, low, largest):
    level = 1.0
    for axis_at, shards_of in cuts:
        heights = jax.random.uniform(jax.random.fold_in(jax.random.fold_in(stream_key, 6), axis_at), (shards_of,), jnp.float32, low / len(cuts), largest / len(cuts))
        level = level * jnp.repeat(jnp.exp(heights), dims[axis_at] // shards_of).reshape((-1,) + (1,) * (len(dims) - 1 - axis_at))
    return level


def centred(key, dims, deviation, reach, shards=(), held_as=jnp.bfloat16):
    values = deviation * jax.random.normal(key, dims, jnp.float32)
    if shards:
        values = values * block_scale(key, dims, shards, -0.22, 0.18)
    return jnp.clip(values, -reach, reach).astype(held_as)


def setup_inputs(seed: int = 0) -> dict:
    streams_of = jax.random.split(jax.random.key(seed), 7)
    control = draw_control(jax.random.fold_in(streams_of[6], 71), 0)
    ensemble = centred(streams_of[1], (MEMBERS, NLAT, NLON, LV), 0.5, 3.0, ((0, 2), (1, 4), (2, 4)))
    precision = jnp.clip(jnp.exp(math.log(8.0) - 2.7725887 * jax.random.uniform(streams_of[2], (NLAT, NLON, LV), jnp.float32) ** block_scale(streams_of[2], (NLAT, NLON, LV), ((0, 4), (1, 4)), -0.2, 0.2)), 0.5, 8.0)
    lat_taps = jnp.clip(jnp.exp(jax.random.uniform(streams_of[3], (TAPS,), jnp.float32, math.log(0.05), math.log(0.3))), 0.05, 0.3)
    lon_taps = jnp.clip(jnp.exp(jax.random.uniform(streams_of[4], (TAPS,), jnp.float32, math.log(0.05), math.log(0.3))), 0.05, 0.3)
    vertical = centred(streams_of[5], (LV, LV), LV ** -0.5, 0.5)
    return dict(control=control, ensemble=ensemble, precision=precision, lat_taps=lat_taps, lon_taps=lon_taps, vertical=vertical)


def smooth_member(values, first_taps, second_taps):
    padded = jnp.pad(values, ((4, 4), (0, 0), (0, 0)))
    padded = jnp.concatenate([padded[:, -4:], padded, padded[:, :4]], axis=1)
    across = first_taps[0] * padded[0:NLAT]
    for offset in range(1, TAPS):
        across = across + first_taps[offset] * padded[offset:offset + NLAT]
    result = second_taps[0] * across[:, 0:NLON]
    for offset in range(1, TAPS):
        result = result + second_taps[offset] * across[:, offset:offset + NLON]
    return result


def reference(control, ensemble, precision, lat_taps, lon_taps, vertical):
    def forward(running, inputs):
        member, spread = inputs
        smoothed = smooth_member(member, lat_taps, lon_taps).astype(jnp.bfloat16)
        leveled = jnp.dot(smoothed.reshape(-1, LV), vertical, preferred_element_type=jnp.float32).reshape(smoothed.shape)
        return running + spread * leveled, None

    increment, unused = lax.scan(forward, jnp.zeros((NLAT, NLON, LV), jnp.float32), (control, ensemble))
    weighted = precision * increment

    def adjoint(inputs):
        member, spread = inputs
        member_part = (spread * weighted).astype(jnp.bfloat16)
        adjoint_lev = jnp.dot(member_part.reshape(-1, LV), vertical.T, preferred_element_type=jnp.float32)
        adjoint_lev = adjoint_lev.reshape(member_part.shape).astype(jnp.bfloat16)
        back = smooth_member(adjoint_lev, lat_taps[::-1], lon_taps[::-1])
        hessian = member + back
        return hessian, jnp.sum(member * hessian)

    hessian, terms = lax.map(adjoint, (control, ensemble))
    curvature = jnp.sum(terms) / (MEMBERS * NLAT * NLON * LV)
    return hessian, curvature
```

```python
import functools

import jax
import jax.numpy as jnp
from jax import lax
from jax.experimental import pallas as pl
from jax.experimental.pallas import tpu as pltpu
from jax.sharding import PartitionSpec as P

F32 = jnp.float32
BF16 = jnp.bfloat16
HALF = 4


def iota(shape, dim):
    return lax.broadcasted_iota(jnp.int32, shape, dim)


def filter_matrix(lat_taps, lon_taps, cols, reverse):
    taps = lat_taps.shape[0]
    shape = (HALF * cols, 3 * HALF * cols + 6 * HALF * HALF)
    out, src = iota(shape, 0), iota(shape, 1)
    main = 3 * HALF * cols
    side = 3 * HALF * HALF
    inside = src < main
    left = src < main + side
    packed = jnp.where(left, src - main, src - main - side)
    row = jnp.where(inside, src // cols, packed // HALF)
    col = jnp.where(
        inside, src % cols, packed % HALF + jnp.where(left, -HALF, cols)
    )
    down = row - out // cols
    across = col - out % cols + HALF
    first = jnp.zeros(shape, F32)
    second = jnp.zeros(shape, F32)
    for tap in range(taps):
        at = taps - 1 - tap if reverse else tap
        first = jnp.where(down == tap, lat_taps[at], first)
        second = jnp.where(across == tap, lon_taps[at], second)
    full = first * second
    high = full.astype(BF16)
    low = (full - high.astype(F32)).astype(BF16)
    return jnp.concatenate([high, low], axis=0)


def pack_matrix(cols):
    size = HALF * HALF
    shape = (2 * size, HALF * cols)
    out, src = iota(shape, 0), iota(shape, 1)
    place = out % size
    col = place % HALF + jnp.where(out < size, 0, cols - HALF)
    wanted = (place // HALF) * cols + col
    return jnp.where(src == wanted, 1.0, 0.0).astype(BF16)


def dot(a, b):
    return jnp.dot(a, b, preferred_element_type=F32)


def kernel(
    axes, sizes, entries, chunks, lat_taps, lon_taps, control, ensemble, precision, vertical, hess, curv,
    ext, ext2, ens, prec, own, inc_out, inc_in, halo, halo2, stage, stage2,
    filt, filt2, picks, vert, vert2, vert2t, sums, cs0, cs1, cs2,
    local_sem, send_sem, recv_sem, inc_send, inc_recv, cs_send, cs_recv,
):
    members, rows, cols, levels = control.shape
    groups = rows // HALF
    cells = HALF * cols
    width = 2 if members % 2 == 0 else 1
    me = {a: lax.axis_index(a) for a in axes}
    n = dict(zip(axes, sizes))

    def device(**at):
        return tuple(at.get(a, me[a]) for a in axes)

    lat, lon = me["lat"], me["lon"]
    left = lax.rem(lon + n["lon"] - 1, n["lon"])
    right = lax.rem(lon + 1, n["lon"])
    has_up = lat > 0
    has_down = lat < n["lat"] - 1

    loads = [
        pltpu.make_async_copy(control, ext.at[:, pl.ds(HALF, rows)], local_sem.at[0]),
        pltpu.make_async_copy(vertical, vert, local_sem.at[1]),
        pltpu.make_async_copy(ensemble, ens, local_sem.at[2]),
        pltpu.make_async_copy(precision, prec, local_sem.at[3]),
    ]
    for load in loads:
        load.start()

    barrier = pltpu.get_barrier_semaphore()
    fixed = 0
    for axis in axes:
        for step in range(1, n[axis]):
            to = device(**{axis: lax.rem(me[axis] + step, n[axis])})
            pl.semaphore_signal(barrier, inc=1, device_id=to, device_id_type=pl.DeviceIdType.MESH)
            fixed += 1
    for has, row in ((has_up, lat - 1), (has_down, lat + 1)):
        @pl.when(has)
        def _():
            for col in (left, right):
                pl.semaphore_signal(
                    barrier, inc=1, device_id=device(lat=row, lon=col), device_id_type=pl.DeviceIdType.MESH
                )
    corners = jnp.where(has_up, 2, 0) + jnp.where(has_down, 2, 0)
    pl.semaphore_wait(barrier, fixed + corners)

    def remote(src, dst, send, recv, to):
        return pltpu.make_async_remote_copy(
            src_ref=src, dst_ref=dst, send_sem=send, recv_sem=recv,
            device_id=to, device_id_type=pl.DeviceIdType.MESH,
        )

    def row_copies(phase, up_src, down_src, dst):
        up = remote(
            up_src, dst.at[:, pl.ds(rows + HALF, HALF)],
            send_sem.at[phase, 0], recv_sem.at[phase, 0], device(lat=lat - 1),
        )
        down = remote(
            down_src, dst.at[:, pl.ds(0, HALF)],
            send_sem.at[phase, 1], recv_sem.at[phase, 1], device(lat=lat + 1),
        )
        return [up], [down]

    def side_copies(phase, src, dst):
        flat, up, down = [], [], []
        for side, to in ((0, left), (1, right)):
            there = dst.at[1 - side]
            mine = src.at[side]
            flat.append(remote(
                mine, there.at[:, pl.ds(1, groups)],
                send_sem.at[phase, 2 + side], recv_sem.at[phase, 2 + side], device(lon=to),
            ))
            up.append(remote(
                mine.at[:, 0], there.at[:, groups + 1],
                send_sem.at[phase, 4 + side], recv_sem.at[phase, 4 + side], device(lat=lat - 1, lon=to),
            ))
            down.append(remote(
                mine.at[:, groups - 1], there.at[:, 0],
                send_sem.at[phase, 6 + side], recv_sem.at[phase, 6 + side], device(lat=lat + 1, lon=to),
            ))
        return flat, up, down

    def start(flat, up, down):
        @pl.when(has_up)
        def _():
            for copy in up:
                copy.start()

        @pl.when(has_down)
        def _():
            for copy in down:
                copy.start()

        for copy in flat:
            copy.start()

    def received(flat, up, down):
        @pl.when(has_up)
        def _():
            for copy in down:
                copy.wait_recv()

        @pl.when(has_down)
        def _():
            for copy in up:
                copy.wait_recv()

        for copy in flat:
            copy.wait_recv()

    def sent(flat, up, down):
        @pl.when(has_up)
        def _():
            for copy in up:
                copy.wait_send()

        @pl.when(has_down)
        def _():
            for copy in down:
                copy.wait_send()

        for copy in flat:
            copy.wait_send()

    row_up, row_down = row_copies(
        0, control.at[:, pl.ds(0, HALF)], control.at[:, pl.ds(rows - HALF, HALF)], ext
    )
    start([], row_up, row_down)

    @pl.when(jnp.logical_not(has_up))
    def _():
        for one, two in ((ext, halo), (ext2, halo2)):
            one[:, 0:HALF] = jnp.zeros((members, HALF, cols, levels), BF16)
            for side in range(2):
                two[side, :, 0] = jnp.zeros((members, HALF * HALF, levels), BF16)

    @pl.when(jnp.logical_not(has_down))
    def _():
        for one, two in ((ext, halo), (ext2, halo2)):
            one[:, rows + HALF : rows + 2 * HALF] = jnp.zeros((members, HALF, cols, levels), BF16)
            for side in range(2):
                two[side, :, groups + 1] = jnp.zeros((members, HALF * HALF, levels), BF16)

    picks[...] = pack_matrix(cols)
    loads[0].wait()

    def pack(blocks, go, dst):
        packed = dot(picks[...], jnp.concatenate(blocks, axis=1)).astype(BF16)
        size = HALF * HALF
        for m in range(members):
            lanes = slice(m * levels, (m + 1) * levels)
            dst[0, m, go] = packed[:size, lanes]
            dst[1, m, go] = packed[size:, lanes]

    def pack_group(go, carry):
        at = pl.ds(HALF * (go + 1), HALF)
        pack([ext[m, at].reshape(cells, levels) for m in range(members)], go, stage)
        return carry

    lax.fori_loop(0, groups, pack_group, 0, unroll=2)
    side_flat, side_up, side_down = side_copies(0, stage, halo)
    start(side_flat, side_up, side_down)

    filt[...] = filter_matrix(lat_taps, lon_taps, cols, False)
    filt2[...] = filter_matrix(lat_taps, lon_taps, cols, True)
    loads[1].wait()
    v = vert[...].astype(F32)
    vt = v.T
    blank = jnp.zeros((levels, levels), F32)

    def diagonal(block):
        if width == 1:
            return block.astype(BF16)
        return jnp.concatenate(
            [jnp.concatenate([block, blank], axis=1), jnp.concatenate([blank, block], axis=1)], axis=0
        ).astype(BF16)

    vert2[...] = diagonal(v)
    vert2t[...] = diagonal(vt)
    sums[...] = jnp.zeros_like(sums)
    loads[2].wait()
    loads[3].wait()

    def tile_sum(x):
        return jnp.sum(x.reshape(-1, 8, levels), axis=0)

    def smooth(source, sides, matrix, go, pair):
        blocks = []
        for m in pair:
            blocks.append(jnp.concatenate([
                source[m, pl.ds(HALF * go, 3 * HALF)].reshape(3 * cells, levels),
                sides[0, m, pl.ds(go, 3)].reshape(3 * HALF * HALF, levels),
                sides[1, m, pl.ds(go, 3)].reshape(3 * HALF * HALF, levels),
            ], axis=0))
        both = dot(matrix[...], jnp.concatenate(blocks, axis=1))
        return both[:cells] + both[cells:]

    pairs = [tuple(range(m, m + width)) for m in range(0, members, width)]

    def forward(go, carry):
        total = None
        for pair in pairs:
            level = dot(smooth(ext, halo, filt, go, pair).astype(BF16), vert2[...])
            for j, m in enumerate(pair):
                spread = ens[m, pl.ds(HALF * go, HALF)].reshape(cells, levels).astype(F32)
                term = spread * level[:, j * levels : (j + 1) * levels]
                total = term if total is None else total + term
        own[go] = total
        inc_out[go] = total.astype(BF16)
        return carry

    received(side_flat, row_up + side_up, row_down + side_down)

    peers = n["mem"] - 1
    per = groups // chunks
    inc_copies = []
    for chunk in range(chunks):
        at = pl.ds(chunk * per, per)
        lax.fori_loop(chunk * per, (chunk + 1) * per, forward, 0, unroll=2)
        copies = []
        for step in range(1, n["mem"]):
            to = device(mem=lax.rem(me["mem"] + step, n["mem"]))
            copies.append(remote(
                inc_out.at[at], inc_in.at[step - 1, at],
                inc_send.at[step - 1, chunk], inc_recv.at[step - 1, chunk], to,
            ))
            copies[-1].start()
        inc_copies.append(copies)

    def squares(go, carry):
        total = sums[...]
        for m in range(members):
            block = ext[m, pl.ds(HALF * (go + 1), HALF)].reshape(cells, levels).astype(F32)
            total = total + tile_sum(block * block)
        sums[...] = total
        return carry

    lax.fori_loop(0, groups, squares, 0)

    def adjoint(go, carry):
        increment = own[go]
        for peer in range(peers):
            increment = increment + inc_in[peer, go].astype(F32)
        weighted = prec[pl.ds(HALF * go, HALF)].reshape(cells, levels) * increment
        sums[...] += tile_sum(weighted * increment) * (1.0 / n["mem"])
        blocks = []
        for pair in pairs:
            parts = []
            for m in pair:
                spread = ens[m, pl.ds(HALF * go, HALF)].reshape(cells, levels).astype(F32)
                parts.append((spread * weighted).astype(BF16))
            result = dot(jnp.concatenate(parts, axis=1), vert2t[...]).astype(BF16)
            for j, m in enumerate(pair):
                block = result[:, j * levels : (j + 1) * levels]
                ext2[m, pl.ds(HALF * (go + 1), HALF)] = block.reshape(HALF, cols, levels)
                blocks.append(block)
        pack(blocks, go, stage2)
        return carry

    for chunk in range(chunks):
        for copy in inc_copies[chunk]:
            copy.wait_recv()
        lax.fori_loop(chunk * per, (chunk + 1) * per, adjoint, 0, unroll=2)

    row2_up, row2_down = row_copies(
        1, ext2.at[:, pl.ds(HALF, HALF)], ext2.at[:, pl.ds(rows, HALF)], ext2
    )
    side2_flat, side2_up, side2_down = side_copies(1, stage2, halo2)
    start(side2_flat, row2_up + side2_up, row2_down + side2_down)

    def final(go, carry):
        for pair in pairs:
            back = smooth(ext2, halo2, filt2, go, pair)
            for j, m in enumerate(pair):
                held = ext[m, pl.ds(HALF * (go + 1), HALF)].astype(F32)
                block = back[:, j * levels : (j + 1) * levels].reshape(HALF, cols, levels)
                hess[m, pl.ds(HALF * go, HALF)] = held + block
        return carry

    partial = sums[...]
    for index, (axis, buf) in enumerate(zip(axes, (cs0, cs1, cs2))):
        mine = me[axis]
        buf[mine] = partial
        copies = []
        for step in range(1, n[axis]):
            to = lax.rem(mine + step, n[axis])
            copies.append(remote(
                buf.at[mine], buf.at[mine], cs_send.at[index, step - 1],
                cs_recv.at[index, mine], device(**{axis: to}),
            ))
            copies[-1].start()
        for step in range(1, n[axis]):
            source = lax.rem(mine + step, n[axis])
            remote(
                buf.at[source], buf.at[source], cs_send.at[index, step - 1],
                cs_recv.at[index, source], device(**{axis: source}),
            ).wait_recv()
        for copy in copies:
            copy.wait_send()
        partial = buf[0]
        for other in range(1, n[axis]):
            partial = partial + buf[other]
    curv[0, 0] = jnp.sum(partial) * (1.0 / entries)

    received(side2_flat, row2_up + side2_up, row2_down + side2_down)
    lax.fori_loop(0, groups, final, 0, unroll=2)

    sent(side_flat, row_up + side_up, row_down + side_down)
    sent(side2_flat, row2_up + side2_up, row2_down + side2_down)
    for copies in inc_copies:
        for copy in copies:
            copy.wait_send()


def per_device(axes, sizes, control, ensemble, precision, lat_taps, lon_taps, vertical):
    members, rows, cols, levels = control.shape
    n = dict(zip(axes, sizes))
    groups = rows // HALF
    cells = HALF * cols
    pack = HALF * HALF
    entries = control.size
    for size in sizes:
        entries *= size
    chunks = 4 if groups % 4 == 0 else 1
    width = 2 if members % 2 == 0 else 1
    inner = 3 * cells + 6 * pack
    smem = pl.BlockSpec(memory_space=pltpu.SMEM)
    anyspace = pl.BlockSpec(memory_space=pl.ANY)
    most = max(sizes)
    peers = max(n["mem"] - 1, 1)
    hessian, curvature = pl.pallas_call(
        functools.partial(kernel, axes, sizes, entries, chunks),
        out_shape=(
            jax.ShapeDtypeStruct(control.shape, F32),
            jax.ShapeDtypeStruct((1, 1), F32),
        ),
        in_specs=[smem, smem, anyspace, anyspace, anyspace, anyspace],
        out_specs=(pl.BlockSpec(memory_space=pltpu.VMEM), smem),
        scratch_shapes=[
            pltpu.VMEM((members, rows + 2 * HALF, cols, levels), BF16),
            pltpu.VMEM((members, rows + 2 * HALF, cols, levels), BF16),
            pltpu.VMEM(control.shape, BF16),
            pltpu.VMEM(precision.shape, F32),
            pltpu.VMEM((groups, cells, levels), F32),
            pltpu.VMEM((groups, cells, levels), BF16),
            pltpu.VMEM((peers, groups, cells, levels), BF16),
            pltpu.VMEM((2, members, groups + 2, pack, levels), BF16),
            pltpu.VMEM((2, members, groups + 2, pack, levels), BF16),
            pltpu.VMEM((2, members, groups, pack, levels), BF16),
            pltpu.VMEM((2, members, groups, pack, levels), BF16),
            pltpu.VMEM((2 * cells, inner), BF16),
            pltpu.VMEM((2 * cells, inner), BF16),
            pltpu.VMEM((2 * pack, cells), BF16),
            pltpu.VMEM((levels, levels), BF16),
            pltpu.VMEM((width * levels, width * levels), BF16),
            pltpu.VMEM((width * levels, width * levels), BF16),
            pltpu.VMEM((8, levels), F32),
            pltpu.VMEM((sizes[0], 8, levels), F32),
            pltpu.VMEM((sizes[1], 8, levels), F32),
            pltpu.VMEM((sizes[2], 8, levels), F32),
            pltpu.SemaphoreType.DMA((4,)),
            pltpu.SemaphoreType.DMA((2, 8)),
            pltpu.SemaphoreType.DMA((2, 8)),
            pltpu.SemaphoreType.DMA((peers, chunks)),
            pltpu.SemaphoreType.DMA((peers, chunks)),
            pltpu.SemaphoreType.DMA((len(axes), most)),
            pltpu.SemaphoreType.DMA((len(axes), most)),
        ],
        compiler_params=pltpu.CompilerParams(
            collective_id=0, has_side_effects=True, vmem_limit_bytes=60 * 1024 * 1024
        ),
    )(lat_taps, lon_taps, control, ensemble, precision, vertical)
    return hessian, curvature.reshape(())


def solution(mesh):
    axes = tuple(mesh.axis_names)
    sizes = tuple(mesh.shape[a] for a in axes)
    in_specs = (
        P("mem", "lat", "lon", None),
        P("mem", "lat", "lon", None),
        P("lat", "lon", None),
        P(),
        P(),
        P(),
    )
    out_specs = (P("mem", "lat", "lon", None), P())
    return jax.shard_map(
        functools.partial(per_device, axes, sizes),
        mesh=mesh, in_specs=in_specs, out_specs=out_specs, check_vma=False,
    )
```

```python
import functools

import jax
import jax.numpy as jnp
from jax import lax
from jax.experimental import pallas as pl
from jax.experimental.pallas import tpu as pltpu
from jax.sharding import PartitionSpec as P

F32 = jnp.float32
BF16 = jnp.bfloat16
HALF = 4


def iota(shape, dim):
    return lax.broadcasted_iota(jnp.int32, shape, dim)


def filter_matrix(lat_taps, lon_taps, cols, reverse):
    taps = lat_taps.shape[0]
    shape = (HALF * cols, 3 * HALF * cols + 6 * HALF * HALF)
    out, src = iota(shape, 0), iota(shape, 1)
    main = 3 * HALF * cols
    side = 3 * HALF * HALF
    inside = src < main
    left = src < main + side
    packed = jnp.where(left, src - main, src - main - side)
    row = jnp.where(inside, src // cols, packed // HALF)
    col = jnp.where(
        inside, src % cols, packed % HALF + jnp.where(left, -HALF, cols)
    )
    down = row - out // cols
    across = col - out % cols + HALF
    first = jnp.zeros(shape, F32)
    second = jnp.zeros(shape, F32)
    for tap in range(taps):
        at = taps - 1 - tap if reverse else tap
        first = jnp.where(down == tap, lat_taps[at], first)
        second = jnp.where(across == tap, lon_taps[at], second)
    full = first * second
    high = full.astype(BF16)
    low = (full - high.astype(F32)).astype(BF16)
    return jnp.concatenate([high, low], axis=0)


def pack_matrix(cols):
    size = HALF * HALF
    shape = (2 * size, HALF * cols)
    out, src = iota(shape, 0), iota(shape, 1)
    place = out % size
    col = place % HALF + jnp.where(out < size, 0, cols - HALF)
    wanted = (place // HALF) * cols + col
    return jnp.where(src == wanted, 1.0, 0.0).astype(BF16)


def dot(a, b):
    return jnp.dot(a, b, preferred_element_type=F32)


def kernel(
    axes, sizes, entries, chunks, lat_taps, lon_taps, control, ensemble, precision, vertical, hess, curv,
    ext, ext2, ens, prec, own, inc_out, inc_in, halo, halo2, stage, stage2,
    outs, filt, filt2, picks, vert, vert2, vert2t, sums, cs0, cs1, cs2,
    local_sem, send_sem, recv_sem, side_send, side_recv, inc_send, inc_recv, cs_send, cs_recv, out_sem,
):
    members, rows, cols, levels = control.shape
    groups = rows // HALF
    per = groups // chunks
    cells = HALF * cols
    width = 2 if members % 2 == 0 else 1
    me = {a: lax.axis_index(a) for a in axes}
    n = dict(zip(axes, sizes))

    def device(**at):
        return tuple(at.get(a, me[a]) for a in axes)

    lat, lon = me["lat"], me["lon"]
    left = lax.rem(lon + n["lon"] - 1, n["lon"])
    right = lax.rem(lon + 1, n["lon"])
    has_up = lat > 0
    has_down = lat < n["lat"] - 1

    loads = [
        pltpu.make_async_copy(control, ext.at[:, pl.ds(HALF, rows)], local_sem.at[0]),
        pltpu.make_async_copy(vertical, vert, local_sem.at[1]),
        pltpu.make_async_copy(ensemble, ens, local_sem.at[2]),
        pltpu.make_async_copy(precision, prec, local_sem.at[3]),
    ]
    for load in loads:
        load.start()

    barrier = pltpu.get_barrier_semaphore()
    fixed = 0
    for axis in axes:
        for step in range(1, n[axis]):
            to = device(**{axis: lax.rem(me[axis] + step, n[axis])})
            pl.semaphore_signal(barrier, inc=1, device_id=to, device_id_type=pl.DeviceIdType.MESH)
            fixed += 1
    for has, row in ((has_up, lat - 1), (has_down, lat + 1)):
        @pl.when(has)
        def _():
            for col in (left, right):
                pl.semaphore_signal(
                    barrier, inc=1, device_id=device(lat=row, lon=col), device_id_type=pl.DeviceIdType.MESH
                )
    corners = jnp.where(has_up, 2, 0) + jnp.where(has_down, 2, 0)
    pl.semaphore_wait(barrier, fixed + corners)

    def remote(src, dst, send, recv, to):
        return pltpu.make_async_remote_copy(
            src_ref=src, dst_ref=dst, send_sem=send, recv_sem=recv,
            device_id=to, device_id_type=pl.DeviceIdType.MESH,
        )

    def row_copies(phase, up_src, down_src, dst):
        up = remote(
            up_src, dst.at[:, pl.ds(rows + HALF, HALF)],
            send_sem.at[phase, 0], recv_sem.at[phase, 0], device(lat=lat - 1),
        )
        down = remote(
            down_src, dst.at[:, pl.ds(0, HALF)],
            send_sem.at[phase, 1], recv_sem.at[phase, 1], device(lat=lat + 1),
        )
        return [up], [down]

    def corner_copies(phase, src, dst):
        up, down = [], []
        for side, to in ((0, left), (1, right)):
            there = dst.at[1 - side]
            mine = src.at[side]
            up.append(remote(
                mine.at[:, 0], there.at[:, groups + 1],
                send_sem.at[phase, 2 + side], recv_sem.at[phase, 2 + side], device(lat=lat - 1, lon=to),
            ))
            down.append(remote(
                mine.at[:, groups - 1], there.at[:, 0],
                send_sem.at[phase, 4 + side], recv_sem.at[phase, 4 + side], device(lat=lat + 1, lon=to),
            ))
        return up, down

    def side_copies(phase, src, dst, chunk):
        return [
            remote(
                src.at[side, :, pl.ds(chunk * per, per)], dst.at[1 - side, :, pl.ds(chunk * per + 1, per)],
                side_send.at[phase, side, chunk], side_recv.at[phase, side, chunk], device(lon=to),
            )
            for side, to in ((0, left), (1, right))
        ]

    def inc_copies(chunk):
        at = pl.ds(chunk * per, per)
        return [
            remote(
                inc_out.at[at], inc_in.at[step - 1, at],
                inc_send.at[step - 1, chunk], inc_recv.at[step - 1, chunk],
                device(mem=lax.rem(me["mem"] + step, n["mem"])),
            )
            for step in range(1, n["mem"])
        ]

    def out_copy(chunk):
        at = pl.ds(chunk * per * HALF, per * HALF)
        return pltpu.make_async_copy(outs.at[:, at], hess.at[:, at], out_sem.at[chunk])

    def each(has, copies, act):
        @pl.when(has)
        def _():
            for copy in copies:
                getattr(copy, act)()

    row_up, row_down = row_copies(
        0, control.at[:, pl.ds(0, HALF)], control.at[:, pl.ds(rows - HALF, HALF)], ext
    )
    each(has_up, row_up, "start")
    each(has_down, row_down, "start")

    @pl.when(jnp.logical_not(has_up))
    def _():
        for one, two in ((ext, halo), (ext2, halo2)):
            one[:, 0:HALF] = jnp.zeros((members, HALF, cols, levels), BF16)
            for side in range(2):
                two[side, :, 0] = jnp.zeros((members, HALF * HALF, levels), BF16)

    @pl.when(jnp.logical_not(has_down))
    def _():
        for one, two in ((ext, halo), (ext2, halo2)):
            one[:, rows + HALF : rows + 2 * HALF] = jnp.zeros((members, HALF, cols, levels), BF16)
            for side in range(2):
                two[side, :, groups + 1] = jnp.zeros((members, HALF * HALF, levels), BF16)

    picks[...] = pack_matrix(cols)
    loads[0].wait()

    def pack(blocks, go, dst):
        packed = dot(picks[...], jnp.concatenate(blocks, axis=1)).astype(BF16)
        size = HALF * HALF
        for m in range(members):
            lanes = slice(m * levels, (m + 1) * levels)
            dst[0, m, go] = packed[:size, lanes]
            dst[1, m, go] = packed[size:, lanes]

    def pack_group(go, carry):
        at = pl.ds(HALF * (go + 1), HALF)
        pack([ext[m, at].reshape(cells, levels) for m in range(members)], go, stage)
        return carry

    lax.fori_loop(0, groups, pack_group, 0, unroll=2)
    corner_up, corner_down = corner_copies(0, stage, halo)
    each(has_up, corner_up, "start")
    each(has_down, corner_down, "start")
    for chunk in range(chunks):
        for copy in side_copies(0, stage, halo, chunk):
            copy.start()

    filt[...] = filter_matrix(lat_taps, lon_taps, cols, False)
    filt2[...] = filter_matrix(lat_taps, lon_taps, cols, True)
    loads[1].wait()
    v = vert[...].astype(F32)
    vt = v.T
    blank = jnp.zeros((levels, levels), F32)

    def diagonal(block):
        if width == 1:
            return block.astype(BF16)
        return jnp.concatenate(
            [jnp.concatenate([block, blank], axis=1), jnp.concatenate([blank, block], axis=1)], axis=0
        ).astype(BF16)

    vert2[...] = diagonal(v)
    vert2t[...] = diagonal(vt)
    sums[...] = jnp.zeros_like(sums)

    def tile_sum(x):
        return jnp.sum(x.reshape(-1, 8, levels), axis=0)

    def squares(go, carry):
        total = sums[...]
        for m in range(members):
            block = ext[m, pl.ds(HALF * (go + 1), HALF)].reshape(cells, levels).astype(F32)
            total = total + tile_sum(block * block)
        sums[...] = total
        return carry

    lax.fori_loop(0, groups, squares, 0)
    loads[2].wait()
    loads[3].wait()

    def smooth(source, sides, matrix, go, pair):
        blocks = []
        for m in pair:
            blocks.append(jnp.concatenate([
                source[m, pl.ds(HALF * go, 3 * HALF)].reshape(3 * cells, levels),
                sides[0, m, pl.ds(go, 3)].reshape(3 * HALF * HALF, levels),
                sides[1, m, pl.ds(go, 3)].reshape(3 * HALF * HALF, levels),
            ], axis=0))
        both = dot(matrix[...], jnp.concatenate(blocks, axis=1))
        return both[:cells] + both[cells:]

    pairs = [tuple(range(m, m + width)) for m in range(0, members, width)]

    def forward(go):
        total = None
        for pair in pairs:
            level = dot(smooth(ext, halo, filt, go, pair).astype(BF16), vert2[...])
            for j, m in enumerate(pair):
                spread = ens[m, pl.ds(HALF * go, HALF)].reshape(cells, levels).astype(F32)
                term = spread * level[:, j * levels : (j + 1) * levels]
                total = term if total is None else total + term
        own[go] = total
        inc_out[go] = total.astype(BF16)

    peers = n["mem"] - 1

    def adjoint(go):
        increment = own[go]
        for peer in range(peers):
            increment = increment + inc_in[peer, go].astype(F32)
        weighted = prec[pl.ds(HALF * go, HALF)].reshape(cells, levels) * increment
        sums[...] += tile_sum(weighted * increment) * (1.0 / n["mem"])
        blocks = []
        for pair in pairs:
            parts = []
            for m in pair:
                spread = ens[m, pl.ds(HALF * go, HALF)].reshape(cells, levels).astype(F32)
                parts.append((spread * weighted).astype(BF16))
            result = dot(jnp.concatenate(parts, axis=1), vert2t[...]).astype(BF16)
            for j, m in enumerate(pair):
                block = result[:, j * levels : (j + 1) * levels]
                ext2[m, pl.ds(HALF * (go + 1), HALF)] = block.reshape(HALF, cols, levels)
                blocks.append(block)
        pack(blocks, go, stage2)

    def final(go):
        for pair in pairs:
            back = smooth(ext2, halo2, filt2, go, pair)
            for j, m in enumerate(pair):
                held = ext[m, pl.ds(HALF * (go + 1), HALF)].astype(F32)
                block = back[:, j * levels : (j + 1) * levels].reshape(HALF, cols, levels)
                outs[m, pl.ds(HALF * go, HALF)] = held + block

    def of_chunk(work, chunk):
        for g in range(per):
            work(chunk * per + g)

    def wait_sides(phase, src, dst, chunk):
        for copy in side_copies(phase, src, dst, chunk):
            copy.wait_recv()

    def forward_chunk(chunk, carry):
        of_chunk(forward, chunk)
        for copy in inc_copies(chunk):
            copy.start()
        return carry

    def forward_wait(chunk, carry):
        wait_sides(0, stage, halo, chunk + 1)
        return forward_chunk(chunk, carry)

    each(has_up, row_down + corner_down, "wait_recv")
    each(has_down, row_up + corner_up, "wait_recv")
    wait_sides(0, stage, halo, 0)
    lax.fori_loop(0, chunks - 1, forward_wait, 0)
    forward_chunk(chunks - 1, 0)

    row2_up, row2_down = row_copies(
        1, ext2.at[:, pl.ds(HALF, HALF)], ext2.at[:, pl.ds(rows, HALF)], ext2
    )
    corner2_up, corner2_down = corner_copies(1, stage2, halo2)

    def adjoint_chunk(chunk, carry):
        for copy in inc_copies(chunk):
            copy.wait_recv()
        of_chunk(adjoint, chunk)
        each(jnp.logical_and(has_up, chunk == 0), row2_up + corner2_up, "start")
        each(jnp.logical_and(has_down, chunk == chunks - 1), row2_down + corner2_down, "start")
        for copy in side_copies(1, stage2, halo2, chunk):
            copy.start()
        return carry

    def final_chunk(chunk, carry):
        of_chunk(final, chunk)
        out_copy(chunk).start()
        return carry

    def final_wait(chunk, carry):
        wait_sides(1, stage2, halo2, chunk + 1)
        return final_chunk(chunk, carry)

    lag = min(4, chunks - 2)

    def both_chunks(chunk, carry):
        adjoint_chunk(chunk, carry)
        return final_wait(chunk - lag, carry)

    lax.fori_loop(0, lag + 1, adjoint_chunk, 0)
    wait_sides(1, stage2, halo2, 0)
    wait_sides(1, stage2, halo2, 1)
    lax.fori_loop(lag + 1, chunks, both_chunks, 0)

    bufs = (cs0, cs1, cs2)

    def reduce_copies(index):
        axis, buf = axes[index], bufs[index]
        mine = me[axis]
        out, arrive = [], []
        for step in range(1, n[axis]):
            other = lax.rem(mine + step, n[axis])
            to = device(**{axis: other})
            sem = cs_send.at[index, step - 1]
            out.append(remote(buf.at[mine], buf.at[mine], sem, cs_recv.at[index, mine], to))
            arrive.append(remote(buf.at[other], buf.at[other], sem, cs_recv.at[index, other], to))
        return out, arrive

    def reduce_start(index, partial):
        bufs[index][me[axes[index]]] = partial
        for copy in reduce_copies(index)[0]:
            copy.start()

    def reduce_end(index):
        out, arrive = reduce_copies(index)
        for copy in arrive:
            copy.wait_recv()
        for copy in out:
            copy.wait_send()
        partial = bufs[index][0]
        for other in range(1, n[axes[index]]):
            partial = partial + bufs[index][other]
        return partial

    reduce_start(0, sums[...])
    rest = chunks - lag
    middle = rest + (lag - 1) // 2
    lax.fori_loop(rest, middle, final_wait, 0)
    reduce_start(1, reduce_end(0))
    lax.fori_loop(middle, chunks - 1, final_wait, 0)
    each(has_down, row2_up + corner2_up, "wait_recv")
    final_chunk(chunks - 1, 0)
    reduce_start(2, reduce_end(1))
    each(has_up, row2_down + corner2_down, "wait_recv")
    final_chunk(0, 0)
    curv[0, 0] = jnp.sum(reduce_end(2)) * (1.0 / entries)

    each(has_up, row_up + corner_up + row2_up + corner2_up, "wait_send")
    each(has_down, row_down + corner_down + row2_down + corner2_down, "wait_send")

    def finish(chunk, carry):
        for copy in side_copies(0, stage, halo, chunk) + side_copies(1, stage2, halo2, chunk):
            copy.wait_send()
        for copy in inc_copies(chunk):
            copy.wait_send()
        out_copy(chunk).wait()
        return carry

    lax.fori_loop(0, chunks, finish, 0)


def per_device(axes, sizes, control, ensemble, precision, lat_taps, lon_taps, vertical):
    members, rows, cols, levels = control.shape
    n = dict(zip(axes, sizes))
    groups = rows // HALF
    cells = HALF * cols
    pack = HALF * HALF
    entries = control.size
    for size in sizes:
        entries *= size
    chunks = next(c for c in (8, 4, groups) if groups % c == 0)
    width = 2 if members % 2 == 0 else 1
    inner = 3 * cells + 6 * pack
    smem = pl.BlockSpec(memory_space=pltpu.SMEM)
    anyspace = pl.BlockSpec(memory_space=pl.ANY)
    most = max(sizes)
    peers = max(n["mem"] - 1, 1)
    hessian, curvature = pl.pallas_call(
        functools.partial(kernel, axes, sizes, entries, chunks),
        out_shape=(
            jax.ShapeDtypeStruct(control.shape, F32),
            jax.ShapeDtypeStruct((1, 1), F32),
        ),
        in_specs=[smem, smem, anyspace, anyspace, anyspace, anyspace],
        out_specs=(anyspace, smem),
        scratch_shapes=[
            pltpu.VMEM((members, rows + 2 * HALF, cols, levels), BF16),
            pltpu.VMEM((members, rows + 2 * HALF, cols, levels), BF16),
            pltpu.VMEM(control.shape, BF16),
            pltpu.VMEM(precision.shape, F32),
            pltpu.VMEM((groups, cells, levels), F32),
            pltpu.VMEM((groups, cells, levels), BF16),
            pltpu.VMEM((peers, groups, cells, levels), BF16),
            pltpu.VMEM((2, members, groups + 2, pack, levels), BF16),
            pltpu.VMEM((2, members, groups + 2, pack, levels), BF16),
            pltpu.VMEM((2, members, groups, pack, levels), BF16),
            pltpu.VMEM((2, members, groups, pack, levels), BF16),
            pltpu.VMEM(control.shape, F32),
            pltpu.VMEM((2 * cells, inner), BF16),
            pltpu.VMEM((2 * cells, inner), BF16),
            pltpu.VMEM((2 * pack, cells), BF16),
            pltpu.VMEM((levels, levels), BF16),
            pltpu.VMEM((width * levels, width * levels), BF16),
            pltpu.VMEM((width * levels, width * levels), BF16),
            pltpu.VMEM((8, levels), F32),
            pltpu.VMEM((sizes[0], 8, levels), F32),
            pltpu.VMEM((sizes[1], 8, levels), F32),
            pltpu.VMEM((sizes[2], 8, levels), F32),
            pltpu.SemaphoreType.DMA((4,)),
            pltpu.SemaphoreType.DMA((2, 6)),
            pltpu.SemaphoreType.DMA((2, 6)),
            pltpu.SemaphoreType.DMA((2, 2, chunks)),
            pltpu.SemaphoreType.DMA((2, 2, chunks)),
            pltpu.SemaphoreType.DMA((peers, chunks)),
            pltpu.SemaphoreType.DMA((peers, chunks)),
            pltpu.SemaphoreType.DMA((len(axes), most)),
            pltpu.SemaphoreType.DMA((len(axes), most)),
            pltpu.SemaphoreType.DMA((chunks,)),
        ],
        compiler_params=pltpu.CompilerParams(
            collective_id=0, has_side_effects=True, vmem_limit_bytes=60 * 1024 * 1024
        ),
    )(lat_taps, lon_taps, control, ensemble, precision, vertical)
    return hessian, curvature.reshape(())


def solution(mesh):
    axes = tuple(mesh.axis_names)
    sizes = tuple(mesh.shape[a] for a in axes)
    in_specs = (
        P("mem", "lat", "lon", None),
        P("mem", "lat", "lon", None),
        P("lat", "lon", None),
        P(),
        P(),
        P(),
    )
    out_specs = (P("mem", "lat", "lon", None), P())
    return jax.shard_map(
        functools.partial(per_device, axes, sizes),
        mesh=mesh, in_specs=in_specs, out_specs=out_specs, check_vma=False,
    )
```

```python
import functools

import jax
import jax.numpy as jnp
from jax import lax
from jax.experimental import pallas as pl
from jax.experimental.pallas import tpu as pltpu
from jax.sharding import PartitionSpec as P

F32 = jnp.float32
BF16 = jnp.bfloat16
HALF = 4


def iota(shape, dim):
    return lax.broadcasted_iota(jnp.int32, shape, dim)


def filter_matrix(lat_taps, lon_taps, cols, reverse):
    taps = lat_taps.shape[0]
    shape = (HALF * cols, 3 * HALF * cols + 6 * HALF * HALF)
    out, src = iota(shape, 0), iota(shape, 1)
    main = 3 * HALF * cols
    side = 3 * HALF * HALF
    inside = src < main
    left = src < main + side
    packed = jnp.where(left, src - main, src - main - side)
    row = jnp.where(inside, src // cols, packed // HALF)
    col = jnp.where(
        inside, src % cols, packed % HALF + jnp.where(left, -HALF, cols)
    )
    down = row - out // cols
    across = col - out % cols + HALF
    first = jnp.zeros(shape, F32)
    second = jnp.zeros(shape, F32)
    for tap in range(taps):
        at = taps - 1 - tap if reverse else tap
        first = jnp.where(down == tap, lat_taps[at], first)
        second = jnp.where(across == tap, lon_taps[at], second)
    full = first * second
    high = full.astype(BF16)
    low = (full - high.astype(F32)).astype(BF16)
    return jnp.concatenate([high, low], axis=0)


def pack_matrix(cols):
    size = HALF * HALF
    shape = (2 * size, HALF * cols)
    out, src = iota(shape, 0), iota(shape, 1)
    place = out % size
    col = place % HALF + jnp.where(out < size, 0, cols - HALF)
    wanted = (place // HALF) * cols + col
    return jnp.where(src == wanted, 1.0, 0.0).astype(BF16)


def dot(a, b):
    return jnp.dot(a, b, preferred_element_type=F32)


def kernel(
    axes, sizes, entries, chunks, lat_taps, lon_taps, control, ensemble, precision, vertical, hess, curv,
    ext, ext2, ens, prec, own, inc_out, inc_in, halo, halo2, stage, stage2,
    filt, filt2, picks, vert, vert2, vert2t, sums, cs0, cs1, cs2,
    local_sem, send_sem, recv_sem, side_send, side_recv, inc_send, inc_recv, cs_send, cs_recv,
):
    members, rows, cols, levels = control.shape
    groups = rows // HALF
    per = groups // chunks
    cells = HALF * cols
    width = 2 if members % 2 == 0 else 1
    me = {a: lax.axis_index(a) for a in axes}
    n = dict(zip(axes, sizes))

    def device(**at):
        return tuple(at.get(a, me[a]) for a in axes)

    lat, lon = me["lat"], me["lon"]
    left = lax.rem(lon + n["lon"] - 1, n["lon"])
    right = lax.rem(lon + 1, n["lon"])
    has_up = lat > 0
    has_down = lat < n["lat"] - 1

    loads = [
        pltpu.make_async_copy(control, ext.at[:, pl.ds(HALF, rows)], local_sem.at[0]),
        pltpu.make_async_copy(vertical, vert, local_sem.at[1]),
        pltpu.make_async_copy(ensemble, ens, local_sem.at[2]),
        pltpu.make_async_copy(precision, prec, local_sem.at[3]),
    ]
    for load in loads:
        load.start()

    barrier = pltpu.get_barrier_semaphore()
    fixed = 0
    for axis in axes:
        for step in range(1, n[axis]):
            to = device(**{axis: lax.rem(me[axis] + step, n[axis])})
            pl.semaphore_signal(barrier, inc=1, device_id=to, device_id_type=pl.DeviceIdType.MESH)
            fixed += 1
    for has, row in ((has_up, lat - 1), (has_down, lat + 1)):
        @pl.when(has)
        def _():
            for col in (left, right):
                pl.semaphore_signal(
                    barrier, inc=1, device_id=device(lat=row, lon=col), device_id_type=pl.DeviceIdType.MESH
                )
    corners = jnp.where(has_up, 2, 0) + jnp.where(has_down, 2, 0)
    pl.semaphore_wait(barrier, fixed + corners)

    def remote(src, dst, send, recv, to):
        return pltpu.make_async_remote_copy(
            src_ref=src, dst_ref=dst, send_sem=send, recv_sem=recv,
            device_id=to, device_id_type=pl.DeviceIdType.MESH,
        )

    def row_copies(phase, up_src, down_src, dst):
        up = remote(
            up_src, dst.at[:, pl.ds(rows + HALF, HALF)],
            send_sem.at[phase, 0], recv_sem.at[phase, 0], device(lat=lat - 1),
        )
        down = remote(
            down_src, dst.at[:, pl.ds(0, HALF)],
            send_sem.at[phase, 1], recv_sem.at[phase, 1], device(lat=lat + 1),
        )
        return [up], [down]

    def corner_copies(phase, src, dst):
        up, down = [], []
        for side, to in ((0, left), (1, right)):
            there = dst.at[1 - side]
            mine = src.at[side]
            up.append(remote(
                mine.at[:, 0], there.at[:, groups + 1],
                send_sem.at[phase, 2 + side], recv_sem.at[phase, 2 + side], device(lat=lat - 1, lon=to),
            ))
            down.append(remote(
                mine.at[:, groups - 1], there.at[:, 0],
                send_sem.at[phase, 4 + side], recv_sem.at[phase, 4 + side], device(lat=lat + 1, lon=to),
            ))
        return up, down

    def side_copies(phase, src, dst, chunk):
        return [
            remote(
                src.at[side, :, pl.ds(chunk * per, per)], dst.at[1 - side, :, pl.ds(chunk * per + 1, per)],
                side_send.at[phase, side, chunk], side_recv.at[phase, side, chunk], device(lon=to),
            )
            for side, to in ((0, left), (1, right))
        ]

    def inc_copies(chunk):
        at = pl.ds(chunk * per, per)
        return [
            remote(
                inc_out.at[at], inc_in.at[step - 1, at],
                inc_send.at[step - 1, chunk], inc_recv.at[step - 1, chunk],
                device(mem=lax.rem(me["mem"] + step, n["mem"])),
            )
            for step in range(1, n["mem"])
        ]

    def each(has, copies, act):
        @pl.when(has)
        def _():
            for copy in copies:
                getattr(copy, act)()

    row_up, row_down = row_copies(
        0, control.at[:, pl.ds(0, HALF)], control.at[:, pl.ds(rows - HALF, HALF)], ext
    )
    each(has_up, row_up, "start")
    each(has_down, row_down, "start")

    @pl.when(jnp.logical_not(has_up))
    def _():
        for one, two in ((ext, halo), (ext2, halo2)):
            one[:, 0:HALF] = jnp.zeros((members, HALF, cols, levels), BF16)
            for side in range(2):
                two[side, :, 0] = jnp.zeros((members, HALF * HALF, levels), BF16)

    @pl.when(jnp.logical_not(has_down))
    def _():
        for one, two in ((ext, halo), (ext2, halo2)):
            one[:, rows + HALF : rows + 2 * HALF] = jnp.zeros((members, HALF, cols, levels), BF16)
            for side in range(2):
                two[side, :, groups + 1] = jnp.zeros((members, HALF * HALF, levels), BF16)

    picks[...] = pack_matrix(cols)
    loads[0].wait()

    def pack(blocks, go, dst):
        packed = dot(picks[...], jnp.concatenate(blocks, axis=1)).astype(BF16)
        size = HALF * HALF
        for m in range(members):
            lanes = slice(m * levels, (m + 1) * levels)
            dst[0, m, go] = packed[:size, lanes]
            dst[1, m, go] = packed[size:, lanes]

    def pack_group(go, carry):
        at = pl.ds(HALF * (go + 1), HALF)
        pack([ext[m, at].reshape(cells, levels) for m in range(members)], go, stage)
        return carry

    lax.fori_loop(0, groups, pack_group, 0, unroll=2)
    corner_up, corner_down = corner_copies(0, stage, halo)
    each(has_up, corner_up, "start")
    each(has_down, corner_down, "start")
    for chunk in range(chunks):
        for copy in side_copies(0, stage, halo, chunk):
            copy.start()

    filt[...] = filter_matrix(lat_taps, lon_taps, cols, False)
    filt2[...] = filter_matrix(lat_taps, lon_taps, cols, True)
    loads[1].wait()
    v = vert[...].astype(F32)
    vt = v.T
    blank = jnp.zeros((levels, levels), F32)

    def diagonal(block):
        if width == 1:
            return block.astype(BF16)
        return jnp.concatenate(
            [jnp.concatenate([block, blank], axis=1), jnp.concatenate([blank, block], axis=1)], axis=0
        ).astype(BF16)

    vert2[...] = diagonal(v)
    vert2t[...] = diagonal(vt)
    sums[...] = jnp.zeros_like(sums)

    def tile_sum(x):
        return jnp.sum(x.reshape(-1, 8, levels), axis=0)

    def squares(go, carry):
        total = sums[...]
        for m in range(members):
            block = ext[m, pl.ds(HALF * (go + 1), HALF)].reshape(cells, levels).astype(F32)
            total = total + tile_sum(block * block)
        sums[...] = total
        return carry

    lax.fori_loop(0, groups, squares, 0)
    loads[2].wait()
    loads[3].wait()

    def smooth(source, sides, matrix, go, pair):
        blocks = []
        for m in pair:
            blocks.append(jnp.concatenate([
                source[m, pl.ds(HALF * go, 3 * HALF)].reshape(3 * cells, levels),
                sides[0, m, pl.ds(go, 3)].reshape(3 * HALF * HALF, levels),
                sides[1, m, pl.ds(go, 3)].reshape(3 * HALF * HALF, levels),
            ], axis=0))
        both = dot(matrix[...], jnp.concatenate(blocks, axis=1))
        return both[:cells] + both[cells:]

    pairs = [tuple(range(m, m + width)) for m in range(0, members, width)]

    def forward(go):
        total = None
        for pair in pairs:
            level = dot(smooth(ext, halo, filt, go, pair).astype(BF16), vert2[...])
            for j, m in enumerate(pair):
                spread = ens[m, pl.ds(HALF * go, HALF)].reshape(cells, levels).astype(F32)
                term = spread * level[:, j * levels : (j + 1) * levels]
                total = term if total is None else total + term
        own[go] = total
        inc_out[go] = total.astype(BF16)

    peers = n["mem"] - 1

    def weigh(go):
        increment = own[go]
        for peer in range(peers):
            increment = increment + inc_in[peer, go].astype(F32)
        weighted = prec[pl.ds(HALF * go, HALF)].reshape(cells, levels) * increment
        sums[...] += tile_sum(weighted * increment) * (1.0 / n["mem"])
        own[go] = weighted

    def adjoint(go):
        weighted = own[go]
        blocks = []
        for pair in pairs:
            parts = []
            for m in pair:
                spread = ens[m, pl.ds(HALF * go, HALF)].reshape(cells, levels).astype(F32)
                parts.append((spread * weighted).astype(BF16))
            result = dot(jnp.concatenate(parts, axis=1), vert2t[...]).astype(BF16)
            for j, m in enumerate(pair):
                block = result[:, j * levels : (j + 1) * levels]
                ext2[m, pl.ds(HALF * (go + 1), HALF)] = block.reshape(HALF, cols, levels)
                blocks.append(block)
        pack(blocks, go, stage2)

    def final(go):
        for pair in pairs:
            back = smooth(ext2, halo2, filt2, go, pair)
            for j, m in enumerate(pair):
                held = ext[m, pl.ds(HALF * (go + 1), HALF)].astype(F32)
                block = back[:, j * levels : (j + 1) * levels].reshape(HALF, cols, levels)
                hess[m, pl.ds(HALF * go, HALF)] = held + block

    def of_chunk(work, chunk):
        for g in range(per):
            work(chunk * per + g)

    def wait_sides(phase, src, dst, chunk):
        for copy in side_copies(phase, src, dst, chunk):
            copy.wait_recv()

    def forward_chunk(chunk, carry):
        of_chunk(forward, chunk)
        for copy in inc_copies(chunk):
            copy.start()
        return carry

    def forward_wait(chunk, carry):
        wait_sides(0, stage, halo, chunk + 1)
        return forward_chunk(chunk, carry)

    each(has_up, row_down + corner_down, "wait_recv")
    each(has_down, row_up + corner_up, "wait_recv")
    wait_sides(0, stage, halo, 0)
    lax.fori_loop(0, chunks - 1, forward_wait, 0)
    forward_chunk(chunks - 1, 0)

    row2_up, row2_down = row_copies(
        1, ext2.at[:, pl.ds(HALF, HALF)], ext2.at[:, pl.ds(rows, HALF)], ext2
    )
    corner2_up, corner2_down = corner_copies(1, stage2, halo2)

    def weigh_chunk(chunk, carry):
        for copy in inc_copies(chunk):
            copy.wait_recv()
        of_chunk(weigh, chunk)
        return carry

    def weigh_adjoint(chunk, carry):
        weigh_chunk(chunk, carry)
        return adjoint_chunk(chunk, carry)

    def adjoint_chunk(chunk, carry):
        of_chunk(adjoint, chunk)
        each(jnp.logical_and(has_up, chunk == 0), row2_up + corner2_up, "start")
        each(jnp.logical_and(has_down, chunk == chunks - 1), row2_down + corner2_down, "start")
        for copy in side_copies(1, stage2, halo2, chunk):
            copy.start()
        return carry

    def final_chunk(chunk, carry):
        of_chunk(final, chunk)
        return carry

    def final_wait(chunk, carry):
        wait_sides(1, stage2, halo2, chunk + 1)
        return final_chunk(chunk, carry)

    lag = min(4, chunks - 2)

    def both_chunks(chunk, carry):
        adjoint_chunk(chunk, carry)
        return final_wait(chunk - lag, carry)

    bufs = (cs0, cs1, cs2)

    def reduce_copies(index):
        axis, buf = axes[index], bufs[index]
        mine = me[axis]
        out, arrive = [], []
        for step in range(1, n[axis]):
            other = lax.rem(mine + step, n[axis])
            to = device(**{axis: other})
            sem = cs_send.at[index, step - 1]
            out.append(remote(buf.at[mine], buf.at[mine], sem, cs_recv.at[index, mine], to))
            arrive.append(remote(buf.at[other], buf.at[other], sem, cs_recv.at[index, other], to))
        return out, arrive

    def reduce_start(index, partial):
        bufs[index][me[axes[index]]] = partial
        for copy in reduce_copies(index)[0]:
            copy.start()

    def reduce_end(index):
        out, arrive = reduce_copies(index)
        for copy in arrive:
            copy.wait_recv()
        for copy in out:
            copy.wait_send()
        partial = bufs[index][0]
        for other in range(1, n[axes[index]]):
            partial = partial + bufs[index][other]
        return partial

    lax.fori_loop(0, lag + 1, weigh_adjoint, 0)
    lax.fori_loop(lag + 1, chunks, weigh_chunk, 0)
    reduce_start(0, sums[...])
    wait_sides(1, stage2, halo2, 0)
    wait_sides(1, stage2, halo2, 1)
    lax.fori_loop(lag + 1, chunks, both_chunks, 0)
    reduce_start(1, reduce_end(0))
    rest = chunks - lag
    middle = rest + (lag - 1) // 2 + 1
    lax.fori_loop(rest, middle, final_wait, 0)
    reduce_start(2, reduce_end(1))
    lax.fori_loop(middle, chunks - 1, final_wait, 0)
    each(has_down, row2_up + corner2_up, "wait_recv")
    final_chunk(chunks - 1, 0)
    each(has_up, row2_down + corner2_down, "wait_recv")
    final_chunk(0, 0)
    curv[0, 0] = jnp.sum(reduce_end(2)) * (1.0 / entries)

    each(has_up, row_up + corner_up + row2_up + corner2_up, "wait_send")
    each(has_down, row_down + corner_down + row2_down + corner2_down, "wait_send")

    def finish(chunk, carry):
        for copy in side_copies(0, stage, halo, chunk) + side_copies(1, stage2, halo2, chunk):
            copy.wait_send()
        for copy in inc_copies(chunk):
            copy.wait_send()
        return carry

    lax.fori_loop(0, chunks, finish, 0)


def per_device(axes, sizes, control, ensemble, precision, lat_taps, lon_taps, vertical):
    members, rows, cols, levels = control.shape
    n = dict(zip(axes, sizes))
    groups = rows // HALF
    cells = HALF * cols
    pack = HALF * HALF
    entries = control.size
    for size in sizes:
        entries *= size
    chunks = next(c for c in (8, 4, groups) if groups % c == 0)
    width = 2 if members % 2 == 0 else 1
    inner = 3 * cells + 6 * pack
    smem = pl.BlockSpec(memory_space=pltpu.SMEM)
    anyspace = pl.BlockSpec(memory_space=pltpu.HBM)
    most = max(sizes)
    peers = max(n["mem"] - 1, 1)
    hessian, curvature = pl.pallas_call(
        functools.partial(kernel, axes, sizes, entries, chunks),
        out_shape=(
            pltpu.VMEM(control.shape, F32),
            jax.ShapeDtypeStruct((1, 1), F32),
        ),
        in_specs=[smem, smem, anyspace, anyspace, anyspace, anyspace],
        out_specs=(pl.BlockSpec(memory_space=pltpu.VMEM), smem),
        scratch_shapes=[
            pltpu.VMEM((members, rows + 2 * HALF, cols, levels), BF16),
            pltpu.VMEM((members, rows + 2 * HALF, cols, levels), BF16),
            pltpu.VMEM(control.shape, BF16),
            pltpu.VMEM(precision.shape, F32),
            pltpu.VMEM((groups, cells, levels), F32),
            pltpu.VMEM((groups, cells, levels), BF16),
            pltpu.VMEM((peers, groups, cells, levels), BF16),
            pltpu.VMEM((2, members, groups + 2, pack, levels), BF16),
            pltpu.VMEM((2, members, groups + 2, pack, levels), BF16),
            pltpu.VMEM((2, members, groups, pack, levels), BF16),
            pltpu.VMEM((2, members, groups, pack, levels), BF16),
            pltpu.VMEM((2 * cells, inner), BF16),
            pltpu.VMEM((2 * cells, inner), BF16),
            pltpu.VMEM((2 * pack, cells), BF16),
            pltpu.VMEM((levels, levels), BF16),
            pltpu.VMEM((width * levels, width * levels), BF16),
            pltpu.VMEM((width * levels, width * levels), BF16),
            pltpu.VMEM((8, levels), F32),
            pltpu.VMEM((sizes[0], 8, levels), F32),
            pltpu.VMEM((sizes[1], 8, levels), F32),
            pltpu.VMEM((sizes[2], 8, levels), F32),
            pltpu.SemaphoreType.DMA((4,)),
            pltpu.SemaphoreType.DMA((2, 6)),
            pltpu.SemaphoreType.DMA((2, 6)),
            pltpu.SemaphoreType.DMA((2, 2, chunks)),
            pltpu.SemaphoreType.DMA((2, 2, chunks)),
            pltpu.SemaphoreType.DMA((peers, chunks)),
            pltpu.SemaphoreType.DMA((peers, chunks)),
            pltpu.SemaphoreType.DMA((len(axes), most)),
            pltpu.SemaphoreType.DMA((len(axes), most)),
        ],
        compiler_params=pltpu.CompilerParams(
            collective_id=0, has_side_effects=True, vmem_limit_bytes=59 * 1024 * 1024
        ),
    )(lat_taps, lon_taps, control, ensemble, precision, vertical)
    return hessian, curvature.reshape(())


def solution(mesh):
    axes = tuple(mesh.axis_names)
    sizes = tuple(mesh.shape[a] for a in axes)
    in_specs = (
        P("mem", "lat", "lon", None),
        P("mem", "lat", "lon", None),
        P("lat", "lon", None),
        P(),
        P(),
        P(),
    )
    out_specs = (P("mem", "lat", "lon", None), P())
    return jax.shard_map(
        functools.partial(per_device, axes, sizes),
        mesh=mesh, in_specs=in_specs, out_specs=out_specs, check_vma=False,
    )
```

```python
import functools

import jax
import jax.numpy as jnp
from jax import lax
from jax.experimental import pallas as pl
from jax.experimental.pallas import tpu as pltpu
from jax.sharding import PartitionSpec as P

F32 = jnp.float32
BF16 = jnp.bfloat16
HALF = 4


def iota(shape, dim):
    return lax.broadcasted_iota(jnp.int32, shape, dim)


def filter_matrix(lat_taps, lon_taps, cols, reverse):
    taps = lat_taps.shape[0]
    shape = (HALF * cols, 3 * HALF * cols + 6 * HALF * HALF)
    out, src = iota(shape, 0), iota(shape, 1)
    main = 3 * HALF * cols
    side = 3 * HALF * HALF
    inside = src < main
    left = src < main + side
    packed = jnp.where(left, src - main, src - main - side)
    row = jnp.where(inside, src // cols, packed // HALF)
    col = jnp.where(
        inside, src % cols, packed % HALF + jnp.where(left, -HALF, cols)
    )
    down = row - out // cols
    across = col - out % cols + HALF
    first = jnp.zeros(shape, F32)
    second = jnp.zeros(shape, F32)
    for tap in range(taps):
        at = taps - 1 - tap if reverse else tap
        first = jnp.where(down == tap, lat_taps[at], first)
        second = jnp.where(across == tap, lon_taps[at], second)
    full = first * second
    high = full.astype(BF16)
    low = (full - high.astype(F32)).astype(BF16)
    return jnp.concatenate([high, low], axis=0)


def pack_matrix(cols):
    size = HALF * HALF
    shape = (2 * size, HALF * cols)
    out, src = iota(shape, 0), iota(shape, 1)
    place = out % size
    col = place % HALF + jnp.where(out < size, 0, cols - HALF)
    wanted = (place // HALF) * cols + col
    return jnp.where(src == wanted, 1.0, 0.0).astype(BF16)


def dot(a, b):
    return jnp.dot(a, b, preferred_element_type=F32)


def kernel(
    axes, sizes, entries, chunks, lat_taps, lon_taps, control, ensemble, precision, vertical, hess, curv,
    ext, ext2, ens, prec, own, inc_out, inc_in, halo, halo2, stage, stage2,
    filt, filt2, picks, vert, vert2, vert2t, sums, cs0, cs1, cs2,
    local_sem, send_sem, recv_sem, side_send, side_recv, inc_send, inc_recv, cs_send, cs_recv,
):
    members, rows, cols, levels = control.shape
    groups = rows // HALF
    per = groups // chunks
    cells = HALF * cols
    width = 2 if members % 2 == 0 else 1
    me = {a: lax.axis_index(a) for a in axes}
    n = dict(zip(axes, sizes))

    def device(**at):
        return tuple(at.get(a, me[a]) for a in axes)

    lat, lon = me["lat"], me["lon"]
    left = lax.rem(lon + n["lon"] - 1, n["lon"])
    right = lax.rem(lon + 1, n["lon"])
    has_up = lat > 0
    has_down = lat < n["lat"] - 1

    loads = [
        pltpu.make_async_copy(control, ext.at[:, pl.ds(HALF, rows)], local_sem.at[0]),
        pltpu.make_async_copy(vertical, vert, local_sem.at[1]),
        pltpu.make_async_copy(ensemble, ens, local_sem.at[2]),
        pltpu.make_async_copy(precision, prec, local_sem.at[3]),
    ]
    for load in loads:
        load.start()

    barrier = pltpu.get_barrier_semaphore()
    fixed = 0
    for axis in axes:
        for step in range(1, n[axis]):
            to = device(**{axis: lax.rem(me[axis] + step, n[axis])})
            pl.semaphore_signal(barrier, inc=1, device_id=to, device_id_type=pl.DeviceIdType.MESH)
            fixed += 1
    for has, row in ((has_up, lat - 1), (has_down, lat + 1)):
        @pl.when(has)
        def _():
            for col in (left, right):
                pl.semaphore_signal(
                    barrier, inc=1, device_id=device(lat=row, lon=col), device_id_type=pl.DeviceIdType.MESH
                )
    corners = jnp.where(has_up, 2, 0) + jnp.where(has_down, 2, 0)
    pl.semaphore_wait(barrier, fixed + corners)

    def remote(src, dst, send, recv, to):
        return pltpu.make_async_remote_copy(
            src_ref=src, dst_ref=dst, send_sem=send, recv_sem=recv,
            device_id=to, device_id_type=pl.DeviceIdType.MESH,
        )

    def row_copies(phase, up_src, down_src, dst):
        up = remote(
            up_src, dst.at[:, pl.ds(rows + HALF, HALF)],
            send_sem.at[phase, 0], recv_sem.at[phase, 0], device(lat=lat - 1),
        )
        down = remote(
            down_src, dst.at[:, pl.ds(0, HALF)],
            send_sem.at[phase, 1], recv_sem.at[phase, 1], device(lat=lat + 1),
        )
        return [up], [down]

    def corner_copies(phase, src, dst):
        up, down = [], []
        for side, to in ((0, left), (1, right)):
            there = dst.at[1 - side]
            mine = src.at[side]
            up.append(remote(
                mine.at[:, 0], there.at[:, groups + 1],
                send_sem.at[phase, 2 + side], recv_sem.at[phase, 2 + side], device(lat=lat - 1, lon=to),
            ))
            down.append(remote(
                mine.at[:, groups - 1], there.at[:, 0],
                send_sem.at[phase, 4 + side], recv_sem.at[phase, 4 + side], device(lat=lat + 1, lon=to),
            ))
        return up, down

    def side_copies(phase, src, dst, chunk):
        return [
            remote(
                src.at[side, :, pl.ds(chunk * per, per)], dst.at[1 - side, :, pl.ds(chunk * per + 1, per)],
                side_send.at[phase, side, chunk], side_recv.at[phase, side, chunk], device(lon=to),
            )
            for side, to in ((0, left), (1, right))
        ]

    def inc_copies(chunk):
        at = pl.ds(chunk * per, per)
        return [
            remote(
                inc_out.at[at], inc_in.at[step - 1, at],
                inc_send.at[step - 1, chunk], inc_recv.at[step - 1, chunk],
                device(mem=lax.rem(me["mem"] + step, n["mem"])),
            )
            for step in range(1, n["mem"])
        ]

    def each(has, copies, act):
        @pl.when(has)
        def _():
            for copy in copies:
                getattr(copy, act)()

    row_up, row_down = row_copies(
        0, control.at[:, pl.ds(0, HALF)], control.at[:, pl.ds(rows - HALF, HALF)], ext
    )
    each(has_up, row_up, "start")
    each(has_down, row_down, "start")

    @pl.when(jnp.logical_not(has_up))
    def _():
        for one, two in ((ext, halo), (ext2, halo2)):
            one[:, 0:HALF] = jnp.zeros((members, HALF, cols, levels), BF16)
            for side in range(2):
                two[side, :, 0] = jnp.zeros((members, HALF * HALF, levels), BF16)

    @pl.when(jnp.logical_not(has_down))
    def _():
        for one, two in ((ext, halo), (ext2, halo2)):
            one[:, rows + HALF : rows + 2 * HALF] = jnp.zeros((members, HALF, cols, levels), BF16)
            for side in range(2):
                two[side, :, groups + 1] = jnp.zeros((members, HALF * HALF, levels), BF16)

    picks[...] = pack_matrix(cols)
    loads[0].wait()

    def pack(blocks, go, dst):
        packed = dot(picks[...], jnp.concatenate(blocks, axis=1)).astype(BF16)
        size = HALF * HALF
        for m in range(members):
            lanes = slice(m * levels, (m + 1) * levels)
            dst[0, m, go] = packed[:size, lanes]
            dst[1, m, go] = packed[size:, lanes]

    def pack_group(go, carry):
        at = pl.ds(HALF * (go + 1), HALF)
        pack([ext[m, at].reshape(cells, levels) for m in range(members)], go, stage)
        return carry

    lax.fori_loop(0, groups, pack_group, 0, unroll=2)
    corner_up, corner_down = corner_copies(0, stage, halo)
    each(has_up, corner_up, "start")
    each(has_down, corner_down, "start")
    for chunk in range(chunks):
        for copy in side_copies(0, stage, halo, chunk):
            copy.start()

    filt[...] = filter_matrix(lat_taps, lon_taps, cols, False)
    filt2[...] = filter_matrix(lat_taps, lon_taps, cols, True)
    loads[1].wait()
    v = vert[...].astype(F32)
    vt = v.T
    blank = jnp.zeros((levels, levels), F32)

    def diagonal(block):
        if width == 1:
            return block.astype(BF16)
        return jnp.concatenate(
            [jnp.concatenate([block, blank], axis=1), jnp.concatenate([blank, block], axis=1)], axis=0
        ).astype(BF16)

    vert2[...] = diagonal(v)
    vert2t[...] = diagonal(vt)
    sums[...] = jnp.zeros_like(sums)

    def tile_sum(x):
        return jnp.sum(x.reshape(-1, 8, levels), axis=0)

    def squares(go, carry):
        total = sums[...]
        for m in range(members):
            block = ext[m, pl.ds(HALF * (go + 1), HALF)].reshape(cells, levels).astype(F32)
            total = total + tile_sum(block * block)
        sums[...] = total
        return carry

    lax.fori_loop(0, groups, squares, 0)
    loads[2].wait()
    loads[3].wait()

    def smooth(source, sides, matrix, go, pair):
        blocks = []
        for m in pair:
            blocks.append(jnp.concatenate([
                source[m, pl.ds(HALF * go, 3 * HALF)].reshape(3 * cells, levels),
                sides[0, m, pl.ds(go, 3)].reshape(3 * HALF * HALF, levels),
                sides[1, m, pl.ds(go, 3)].reshape(3 * HALF * HALF, levels),
            ], axis=0))
        both = dot(matrix[...], jnp.concatenate(blocks, axis=1))
        return both[:cells] + both[cells:]

    pairs = [tuple(range(m, m + width)) for m in range(0, members, width)]

    def forward(chunk):
        places = [chunk * per + g for g in range(per)]
        smoothed = [[smooth(ext, halo, filt, go, pair).astype(BF16) for pair in pairs] for go in places]
        for go, held in zip(places, smoothed):
            total = None
            for pair, value in zip(pairs, held):
                level = dot(value, vert2[...])
                for j, m in enumerate(pair):
                    spread = ens[m, pl.ds(HALF * go, HALF)].reshape(cells, levels).astype(F32)
                    term = spread * level[:, j * levels : (j + 1) * levels]
                    total = term if total is None else total + term
            own[go] = total
            inc_out[go] = total.astype(BF16)

    peers = n["mem"] - 1

    def weigh(go):
        increment = own[go]
        for peer in range(peers):
            increment = increment + inc_in[peer, go].astype(F32)
        weighted = prec[pl.ds(HALF * go, HALF)].reshape(cells, levels) * increment
        sums[...] += tile_sum(weighted * increment) * (1.0 / n["mem"])
        own[go] = weighted

    def adjoint(go):
        weighted = own[go]
        blocks = []
        for pair in pairs:
            parts = []
            for m in pair:
                spread = ens[m, pl.ds(HALF * go, HALF)].reshape(cells, levels).astype(F32)
                parts.append((spread * weighted).astype(BF16))
            result = dot(jnp.concatenate(parts, axis=1), vert2t[...]).astype(BF16)
            for j, m in enumerate(pair):
                block = result[:, j * levels : (j + 1) * levels]
                ext2[m, pl.ds(HALF * (go + 1), HALF)] = block.reshape(HALF, cols, levels)
                blocks.append(block)
        pack(blocks, go, stage2)

    def final(go):
        for pair in pairs:
            back = smooth(ext2, halo2, filt2, go, pair)
            for j, m in enumerate(pair):
                held = ext[m, pl.ds(HALF * (go + 1), HALF)].astype(F32)
                block = back[:, j * levels : (j + 1) * levels].reshape(HALF, cols, levels)
                hess[m, pl.ds(HALF * go, HALF)] = held + block

    def of_chunk(work, chunk):
        for g in range(per):
            work(chunk * per + g)

    def wait_sides(phase, src, dst, chunk):
        for copy in side_copies(phase, src, dst, chunk):
            copy.wait_recv()

    def forward_chunk(chunk, carry):
        forward(chunk)
        for copy in inc_copies(chunk):
            copy.start()
        return carry

    def forward_wait(chunk, carry):
        wait_sides(0, stage, halo, chunk + 1)
        return forward_chunk(chunk, carry)

    each(has_up, row_down + corner_down, "wait_recv")
    each(has_down, row_up + corner_up, "wait_recv")
    wait_sides(0, stage, halo, 0)
    lax.fori_loop(0, chunks - 1, forward_wait, 0)
    forward_chunk(chunks - 1, 0)

    row2_up, row2_down = row_copies(
        1, ext2.at[:, pl.ds(HALF, HALF)], ext2.at[:, pl.ds(rows, HALF)], ext2
    )
    corner2_up, corner2_down = corner_copies(1, stage2, halo2)

    def weigh_chunk(chunk, carry):
        for copy in inc_copies(chunk):
            copy.wait_recv()
        of_chunk(weigh, chunk)
        return carry

    def weigh_adjoint(chunk, carry):
        weigh_chunk(chunk, carry)
        return adjoint_chunk(chunk, carry)

    def adjoint_chunk(chunk, carry):
        of_chunk(adjoint, chunk)
        each(jnp.logical_and(has_up, chunk == 0), row2_up + corner2_up, "start")
        each(jnp.logical_and(has_down, chunk == chunks - 1), row2_down + corner2_down, "start")
        for copy in side_copies(1, stage2, halo2, chunk):
            copy.start()
        return carry

    def final_chunk(chunk, carry):
        of_chunk(final, chunk)
        return carry

    def final_wait(chunk, carry):
        wait_sides(1, stage2, halo2, chunk + 1)
        return final_chunk(chunk, carry)

    lag = min(4, chunks - 2)

    def both_chunks(chunk, carry):
        adjoint_chunk(chunk, carry)
        return final_wait(chunk - lag, carry)

    bufs = (cs0, cs1, cs2)

    def reduce_copies(index):
        axis, buf = axes[index], bufs[index]
        mine = me[axis]
        out, arrive = [], []
        for step in range(1, n[axis]):
            other = lax.rem(mine + step, n[axis])
            to = device(**{axis: other})
            sem = cs_send.at[index, step - 1]
            out.append(remote(buf.at[mine], buf.at[mine], sem, cs_recv.at[index, mine], to))
            arrive.append(remote(buf.at[other], buf.at[other], sem, cs_recv.at[index, other], to))
        return out, arrive

    def reduce_start(index, partial):
        bufs[index][me[axes[index]]] = partial
        for copy in reduce_copies(index)[0]:
            copy.start()

    def reduce_end(index):
        out, arrive = reduce_copies(index)
        for copy in arrive:
            copy.wait_recv()
        for copy in out:
            copy.wait_send()
        partial = bufs[index][0]
        for other in range(1, n[axes[index]]):
            partial = partial + bufs[index][other]
        return partial

    lax.fori_loop(0, lag + 1, weigh_adjoint, 0)
    lax.fori_loop(lag + 1, chunks, weigh_chunk, 0)
    reduce_start(0, sums[...])
    wait_sides(1, stage2, halo2, 0)
    wait_sides(1, stage2, halo2, 1)
    lax.fori_loop(lag + 1, chunks, both_chunks, 0)
    reduce_start(1, reduce_end(0))
    rest = chunks - lag
    middle = rest + (lag - 1) // 2 + 1
    lax.fori_loop(rest, middle, final_wait, 0)
    reduce_start(2, reduce_end(1))
    lax.fori_loop(middle, chunks - 1, final_wait, 0)
    each(has_down, row2_up + corner2_up, "wait_recv")
    final_chunk(chunks - 1, 0)
    each(has_up, row2_down + corner2_down, "wait_recv")
    final_chunk(0, 0)
    curv[0, 0] = jnp.sum(reduce_end(2)) * (1.0 / entries)

    each(has_up, row_up + corner_up + row2_up + corner2_up, "wait_send")
    each(has_down, row_down + corner_down + row2_down + corner2_down, "wait_send")

    def finish(chunk, carry):
        for copy in side_copies(0, stage, halo, chunk) + side_copies(1, stage2, halo2, chunk):
            copy.wait_send()
        for copy in inc_copies(chunk):
            copy.wait_send()
        return carry

    lax.fori_loop(0, chunks, finish, 0)


def per_device(axes, sizes, control, ensemble, precision, lat_taps, lon_taps, vertical):
    members, rows, cols, levels = control.shape
    n = dict(zip(axes, sizes))
    groups = rows // HALF
    cells = HALF * cols
    pack = HALF * HALF
    entries = control.size
    for size in sizes:
        entries *= size
    chunks = next(c for c in (8, 4, groups) if groups % c == 0)
    width = 2 if members % 2 == 0 else 1
    inner = 3 * cells + 6 * pack
    smem = pl.BlockSpec(memory_space=pltpu.SMEM)
    anyspace = pl.BlockSpec(memory_space=pltpu.HBM)
    most = max(sizes)
    peers = max(n["mem"] - 1, 1)
    hessian, curvature = pl.pallas_call(
        functools.partial(kernel, axes, sizes, entries, chunks),
        out_shape=(
            pltpu.VMEM(control.shape, F32),
            jax.ShapeDtypeStruct((1, 1), F32),
        ),
        in_specs=[smem, smem, anyspace, anyspace, anyspace, anyspace],
        out_specs=(pl.BlockSpec(memory_space=pltpu.VMEM), smem),
        scratch_shapes=[
            pltpu.VMEM((members, rows + 2 * HALF, cols, levels), BF16),
            pltpu.VMEM((members, rows + 2 * HALF, cols, levels), BF16),
            pltpu.VMEM(control.shape, BF16),
            pltpu.VMEM(precision.shape, F32),
            pltpu.VMEM((groups, cells, levels), F32),
            pltpu.VMEM((groups, cells, levels), BF16),
            pltpu.VMEM((peers, groups, cells, levels), BF16),
            pltpu.VMEM((2, members, groups + 2, pack, levels), BF16),
            pltpu.VMEM((2, members, groups + 2, pack, levels), BF16),
            pltpu.VMEM((2, members, groups, pack, levels), BF16),
            pltpu.VMEM((2, members, groups, pack, levels), BF16),
            pltpu.VMEM((2 * cells, inner), BF16),
            pltpu.VMEM((2 * cells, inner), BF16),
            pltpu.VMEM((2 * pack, cells), BF16),
            pltpu.VMEM((levels, levels), BF16),
            pltpu.VMEM((width * levels, width * levels), BF16),
            pltpu.VMEM((width * levels, width * levels), BF16),
            pltpu.VMEM((8, levels), F32),
            pltpu.VMEM((sizes[0], 8, levels), F32),
            pltpu.VMEM((sizes[1], 8, levels), F32),
            pltpu.VMEM((sizes[2], 8, levels), F32),
            pltpu.SemaphoreType.DMA((4,)),
            pltpu.SemaphoreType.DMA((2, 6)),
            pltpu.SemaphoreType.DMA((2, 6)),
            pltpu.SemaphoreType.DMA((2, 2, chunks)),
            pltpu.SemaphoreType.DMA((2, 2, chunks)),
            pltpu.SemaphoreType.DMA((peers, chunks)),
            pltpu.SemaphoreType.DMA((peers, chunks)),
            pltpu.SemaphoreType.DMA((len(axes), most)),
            pltpu.SemaphoreType.DMA((len(axes), most)),
        ],
        compiler_params=pltpu.CompilerParams(
            collective_id=0, has_side_effects=True, vmem_limit_bytes=59 * 1024 * 1024
        ),
    )(lat_taps, lon_taps, control, ensemble, precision, vertical)
    return hessian, curvature.reshape(())


def solution(mesh):
    axes = tuple(mesh.axis_names)
    sizes = tuple(mesh.shape[a] for a in axes)
    in_specs = (
        P("mem", "lat", "lon", None),
        P("mem", "lat", "lon", None),
        P("lat", "lon", None),
        P(),
        P(),
        P(),
    )
    out_specs = (P("mem", "lat", "lon", None), P())
    return jax.shard_map(
        functools.partial(per_device, axes, sizes),
        mesh=mesh, in_specs=in_specs, out_specs=out_specs, check_vma=False,
    )
```
